32 devices in a mesh: dp: 8 (over z, x), tensor: 4 (over y, core).
Axes of the slice: x: 2, y: 2, z: 4, core: 2. Of those that a mesh axis runs over, the one named last changes fastest.
Arguments:
- tokens: bfloat16 [8192, 1536], P(('dp', 'tensor')), may hold values from -6 to 6
- cotangent: bfloat16 [8192, 1536], P(('dp', 'tensor')), may hold values from -6 to 6
- norm1_gain: bfloat16 [1536], P(('dp', 'tensor')), may hold values from 0.5 to 1.5
- query_weight: bfloat16 [1536, 1536], P('dp', 'tensor'), may hold values from -0.15625 to 0.15625
- query_bias: bfloat16 [1536], P(('dp', 'tensor')), may hold values from -3 to 3
- key_weight: bfloat16 [1536, 256], P(('dp', 'tensor')), may hold values from -0.15625 to 0.15625
- key_bias: bfloat16 [256], P(('dp', 'tensor')), may hold values from -3 to 3
- value_weight: bfloat16 [1536, 256], P(('dp', 'tensor')), may hold values from -0.15625 to 0.15625
- value_bias: bfloat16 [256], P(('dp', 'tensor')), may hold values from -3 to 3
- out_weight: bfloat16 [1536, 1536], P('tensor', 'dp'), may hold values from -0.625 to 0.625
- norm2_gain: bfloat16 [1536], P(('dp', 'tensor')), may hold values from 0.5 to 1.5
- gate_weight: bfloat16 [1536, 8960], P('dp', 'tensor'), may hold values from -0.15625 to 0.15625
- up_weight: bfloat16 [1536, 8960], P('dp', 'tensor'), may hold values from -0.15625 to 0.15625
- down_weight: bfloat16 [8960, 1536], P('tensor', 'dp'), may hold values from -0.0625 to 0.0625
Outputs:
- output: float32 [8192, 1536], P(('dp', 'tensor'))
- tokens_grad: float32 [8192, 1536], P(('dp', 'tensor'))
- norm1_gain_grad: float32 [1536], P(('dp', 'tensor'))
- query_weight_grad: float32 [1536, 1536], P('dp', 'tensor')
- query_bias_grad: float32 [1536], P(('dp', 'tensor'))
- key_weight_grad: float32 [1536, 256], P(('dp', 'tensor'))
- key_bias_grad: float32 [256], P(('dp', 'tensor'))
- value_weight_grad: float32 [1536, 256], P(('dp', 'tensor'))
- value_bias_grad: float32 [256], P(('dp', 'tensor'))
- out_weight_grad: float32 [1536, 1536], P('tensor', 'dp')
- norm2_gain_grad: float32 [1536], P(('dp', 'tensor'))
- gate_weight_grad: float32 [1536, 8960], P('dp', 'tensor')
- up_weight_grad: float32 [1536, 8960], P('dp', 'tensor')
- down_weight_grad: float32 [8960, 1536], P('tensor', 'dp')
The draws below stay inside these ranges and needn't reach their ends.
All inputs are finite; a program needn't handle non-finite values.
Results may differ from the reference program's by a relative error of at most 0.024.
Values may be sent and summed in bfloat16 or wider, within the bound.
A program may use at most 192 MiB of HBM per device.

```python
import jax
import jax.numpy as jnp
from jax import lax

D = 1536
H = 12
KV = 2
HD = 128
FF = 8960
SEQ_LEN = 1024
BLOCK = 256
TOKENS = 8192


def level_of(own_key, shape, cuts, least, top_value):
    loudness = 1.0
    for dim, blocks in cuts:
        steps = jax.random.uniform(jax.random.fold_in(jax.random.fold_in(own_key, 6), dim), (blocks,), jnp.float32, least / len(cuts), top_value / len(cuts))
        loudness = loudness * jnp.repeat(jnp.exp(steps), shape[dim] // blocks).reshape((-1,) + (1,) * (len(shape) - 1 - dim))
    return loudness


def bell_draw(rng, extent, deviation, bound, pieces=(), kind=jnp.bfloat16):
    entries = jax.random.normal(rng, extent, jnp.float32) * deviation
    if len(pieces) > 0:
        entries = level_of(rng, extent, pieces, -0.22, 0.18) * entries
    return jnp.clip(entries, min=-bound, max=bound).astype(kind)


def setup_inputs(seed: int = 0) -> dict:
    key_list = jax.random.split(jax.random.key(seed), 15)
    tokens = bell_draw(key_list[0], (TOKENS, D), 1.0, 6.0, ((0, 32),))
    cotangent = bell_draw(key_list[1], (TOKENS, D), 1.0, 6.0, ((0, 32),))
    norm1_gain = jnp.clip(1.0 + 0.1 * jax.random.normal(key_list[2], (D,), jnp.float32), 0.5, 1.5).astype(jnp.bfloat16)
    query_weight = bell_draw(key_list[3], (D, H * HD), D ** -0.5, 0.15625, ((0, 8), (1, 4)))
    query_bias = bell_draw(key_list[4], (H * HD,), 0.5, 3.0, ((0, 32),))
    key_weight = bell_draw(key_list[5], (D, KV * HD), D ** -0.5, 0.15625, ((0, 32),))
    key_bias = bell_draw(key_list[6], (KV * HD,), 0.5, 3.0, ((0, 32),))
    value_weight = bell_draw(key_list[7], (D, KV * HD), D ** -0.5, 0.15625, ((0, 32),))
    value_bias = bell_draw(key_list[8], (KV * HD,), 0.5, 3.0, ((0, 32),))
    out_weight = bell_draw(key_list[9], (H * HD, D), (H * HD // 16) ** -0.5, 0.625, ((0, 4), (1, 8)))
    norm2_gain = jnp.clip(1.0 + 0.1 * jax.random.normal(key_list[10], (D,), jnp.float32), 0.5, 1.5).astype(jnp.bfloat16)
    gate_weight = bell_draw(key_list[11], (D, FF), D ** -0.5, 0.15625, ((0, 8), (1, 4)))
    up_weight = bell_draw(key_list[12], (D, FF), D ** -0.5, 0.15625, ((0, 8), (1, 4)))
    down_weight = bell_draw(key_list[13], (FF, D), FF ** -0.5, 0.0625, ((0, 4), (1, 8)))
    return dict(tokens=tokens, cotangent=cotangent, norm1_gain=norm1_gain, query_weight=query_weight, query_bias=query_bias, key_weight=key_weight, key_bias=key_bias, value_weight=value_weight, value_bias=value_bias, out_weight=out_weight, norm2_gain=norm2_gain, gate_weight=gate_weight, up_weight=up_weight, down_weight=down_weight)


@jax.custom_vjp
def low(v):
    return lax.optimization_barrier(v.astype(jnp.bfloat16)).astype(jnp.float32)

@jax.custom_vjp
def low_back(v):
    return v

def low_keep(v):
    return (low(v), None)

def low_pass(kept, grad):
    return (grad,)

def back_keep(v):
    return (v, None)

def back_low(kept, grad):
    return (low(grad),)
low.defvjp(low_keep, low_pass)
low_back.defvjp(back_keep, back_low)
epsilon = 1e-06
rope_base = 1000000.0

def highest(first_op, second_op):
    return jnp.dot(first_op, second_op, precision=lax.Precision.HIGHEST)

def rms_scale(values, norm_gain):
    return values * lax.rsqrt(lax.optimization_barrier(jnp.mean(values * values, axis=-1, keepdims=True)) + epsilon) * norm_gain

def rotate(field, cosine_table, sine_table):
    half_width = field.shape[-1] // 2
    turned = jnp.concatenate([-field[..., half_width:], field[..., :half_width]], axis=-1)
    return field * cosine_table + turned * sine_table

def rope_tables():
    positions = jnp.arange(SEQ_LEN, dtype=jnp.float32)
    frequency = rope_base ** (-(jnp.arange(HD // 2, dtype=jnp.float32) * 2.0) / HD)
    angles = positions[:, None] * frequency[None, :]
    cosine_table = jnp.concatenate([jnp.cos(angles), jnp.cos(angles)], axis=-1)[:, None, :]
    sine_table = jnp.concatenate([jnp.sin(angles), jnp.sin(angles)], axis=-1)[:, None, :]
    return (cosine_table, sine_table)

def attend(operands):
    query_seq, key_seq, value_seq = operands
    group_size = H // KV
    keys_wide = jnp.repeat(key_seq, group_size, axis=1)
    values_wide = jnp.repeat(value_seq, group_size, axis=1)
    scores = jnp.einsum('qhd,khd->hqk', query_seq, keys_wide, precision=lax.Precision.HIGHEST)
    scores = low_back(scores * HD ** (-0.5))
    block_ids = jnp.arange(SEQ_LEN) // BLOCK
    allowed = block_ids[None, :] <= block_ids[:, None]
    scores = jnp.where(allowed[None], scores, -1e+30)
    row_max = lax.optimization_barrier(jnp.max(scores, axis=-1, keepdims=True))
    exponent = jnp.exp(scores - row_max)
    attn_probs = low(exponent / lax.optimization_barrier(jnp.sum(exponent, axis=-1, keepdims=True)))
    return jnp.einsum('hqk,khd->qhd', attn_probs, values_wide, precision=lax.Precision.HIGHEST)

def block_forward(tokens, norm1_gain, query_weight, query_bias, key_weight, key_bias, value_weight, value_bias, out_weight, norm2_gain, gate_weight, up_weight, down_weight):
    token_count = tokens.shape[0]
    seq_count = token_count // SEQ_LEN
    normed = low(rms_scale(tokens, norm1_gain))
    query_pre = low_back(highest(normed, query_weight)) + query_bias
    key_pre = low_back(highest(normed, key_weight)) + key_bias
    value_pre = low_back(highest(normed, value_weight)) + value_bias
    cosine_table, sine_table = rope_tables()
    query_heads = low(rotate(query_pre.reshape(seq_count, SEQ_LEN, H, HD), cosine_table, sine_table))
    key_heads = low(rotate(key_pre.reshape(seq_count, SEQ_LEN, KV, HD), cosine_table, sine_table))
    value_heads = low(value_pre.reshape(seq_count, SEQ_LEN, KV, HD))
    mixed_heads = lax.map(jax.checkpoint(attend), (query_heads, key_heads, value_heads))
    mixed_heads = low(low_back(mixed_heads.reshape(token_count, H * HD)))
    hidden_one = tokens + low_back(highest(mixed_heads, out_weight))
    normed_two = low(rms_scale(hidden_one, norm2_gain))
    gate_vals = low_back(highest(normed_two, gate_weight))
    up_vals = low_back(highest(normed_two, up_weight))
    activated = low(jax.nn.silu(gate_vals) * up_vals)
    return hidden_one + low_back(highest(activated, down_weight))

def reference(tokens, cotangent, norm1_gain, query_weight, query_bias, key_weight, key_bias, value_weight, value_bias, out_weight, norm2_gain, gate_weight, up_weight, down_weight):
    float_args = [array_in.astype(jnp.float32) for array_in in (tokens, norm1_gain, query_weight, query_bias, key_weight, key_bias, value_weight, value_bias, out_weight, norm2_gain, gate_weight, up_weight, down_weight)]
    output, pullback = jax.vjp(block_forward, *float_args)
    gradients = pullback(cotangent.astype(jnp.float32))
    return (output, gradients[0], gradients[1], gradients[2], gradients[3], gradients[4], gradients[5], gradients[6], gradients[7], gradients[8], gradients[9], gradients[10], gradients[11], gradients[12])
```

```python
import functools

import jax
import jax.numpy as jnp
from jax import lax
from jax.experimental import pallas as pl
from jax.experimental.pallas import tpu as pltpu
from jax.sharding import PartitionSpec as P

H = 12
KV = 2
HD = 128
SEQ_LEN = 1024
BLOCK = 256

epsilon = 1e-06
rope_base = 1000000.0
bf16 = jnp.bfloat16
f32 = jnp.float32


LOW = 1


def swap(value, axis, bit):
    size = lax.axis_size(axis)
    return lax.ppermute(value, axis, [(i, i ^ (1 << bit)) for i in range(size)])


def mm(a, b):
    return jnp.dot(a, b, preferred_element_type=f32)


def mm_tn(a, b):
    return lax.dot_general(a, b, (((0,), (0,)), ((), ())), preferred_element_type=f32)


def mm_nt(a, b):
    return lax.dot_general(a, b, (((1,), (1,)), ((), ())), preferred_element_type=f32)


def pick(value, index, axis):
    return lax.dynamic_index_in_dim(value, index, axis, keepdims=False)


def place(blocks, count, me):
    first = blocks[0][1]
    out = jnp.zeros((count,) + first.shape, first.dtype)
    for offset, block in blocks:
        out = lax.dynamic_update_slice_in_dim(out, block[None], me ^ offset, 0)
    return out


def spread(block, axis, bits):
    held = [(0, block)]
    for bit in bits:
        held = held + [(o ^ (1 << bit), swap(b, axis, bit)) for o, b in held]
    return held


def rope_tables():
    positions = lax.iota(f32, SEQ_LEN)
    frequency = rope_base ** (-(lax.iota(f32, HD // 2) * 2.0) / HD)
    angles = positions[:, None] * frequency[None, :]
    cosine, sine = jnp.cos(angles), jnp.sin(angles)
    return jnp.concatenate([cosine, cosine], -1), jnp.concatenate([-sine, sine], -1)


def attend_kernel(heads, qkv_ref, bias_ref, cos_ref, sin_ref, q_ref, k_ref, v_ref, o_ref, lse_ref):
    factor = HD**-0.5
    cosine, sine = cos_ref[...], sin_ref[...]
    for h in range(heads + 1):
        z = qkv_ref[:, h * HD : (h + 1) * HD] + bias_ref[:, h * HD : (h + 1) * HD]
        z = (z * cosine + pltpu.roll(z, HD // 2, 1) * sine).astype(bf16)
        if h < heads:
            q_ref[:, h * HD : (h + 1) * HD] = z
        else:
            k_ref[...] = z
    last = (heads + 1) * HD
    v_ref[...] = (qkv_ref[:, last : last + HD] + bias_ref[:, last : last + HD]).astype(bf16)
    v_turned = v_ref[...].T
    for i in range(SEQ_LEN // BLOCK):
        rows = slice(i * BLOCK, (i + 1) * BLOCK)
        keys = (i + 1) * BLOCK
        for h in range(heads):
            cols = slice(h * HD, (h + 1) * HD)
            scores = mm_nt(k_ref[:keys, :], q_ref[rows, cols]) * factor
            top = jnp.max(scores, axis=0, keepdims=True)
            grown = jnp.exp(scores - top)
            total = jnp.sum(grown, axis=0, keepdims=True)
            probs = (grown * (1.0 / total)).astype(bf16)
            o_ref[rows, cols] = mm(v_turned[:, :keys], probs).T.astype(bf16)
            lse_ref[h : h + 1, rows] = top + jnp.log(total)


def attend_back_kernel(
    heads, q_ref, k_ref, v_ref, lse_ref, do_ref, cos_ref, sin_ref, d_ref, bias_ref, dk, dv
):
    factor = HD**-0.5
    cosine, sine = cos_ref[...], sin_ref[...]
    k_turned = k_ref[...].T
    dk[...] = jnp.zeros_like(dk)
    dv[...] = jnp.zeros_like(dv)
    qsum = [jnp.zeros((1, HD), f32) for _ in range(heads)]
    for i in range(SEQ_LEN // BLOCK):
        rows = slice(i * BLOCK, (i + 1) * BLOCK)
        keys = (i + 1) * BLOCK
        for h in range(heads):
            cols = slice(h * HD, (h + 1) * HD)
            q, do = q_ref[rows, cols], do_ref[rows, cols]
            scores = mm_nt(k_ref[:keys, :], q) * factor
            probs = jnp.exp(scores - lse_ref[h : h + 1, rows])
            dv[:keys, :] += mm(probs.astype(bf16), do)
            dp = mm_nt(v_ref[:keys, :], do)
            delta = jnp.sum(probs * dp, axis=0, keepdims=True)
            ds = (probs * (dp - delta)).astype(bf16)
            dk[:keys, :] += mm(ds, q)
            w = mm(k_turned[:, :keys], ds).T * factor
            w = w * cosine[rows, :] - pltpu.roll(w, HD // 2, 1) * sine[rows, :]
            qsum[h] = qsum[h] + jnp.sum(w, axis=0, keepdims=True)
            d_ref[rows, cols] = w.astype(bf16)
    for h in range(heads):
        bias_ref[:, h * HD : (h + 1) * HD] = qsum[h]
    w = dk[...] * factor
    w = w * cosine - pltpu.roll(w, HD // 2, 1) * sine
    last = heads * HD
    d_ref[:, last : last + HD] = w.astype(bf16)
    bias_ref[:, last : last + HD] = jnp.sum(w, axis=0, keepdims=True)
    d_ref[:, last + HD : last + 2 * HD] = dv[...].astype(bf16)
    bias_ref[:, last + HD : last + 2 * HD] = jnp.sum(dv[...], axis=0, keepdims=True)


def struct(*shape, dtype=bf16):
    return jax.ShapeDtypeStruct(shape, dtype)


def attend(heads, qkv, bias, cosine, sine):
    n = SEQ_LEN
    return pl.pallas_call(
        functools.partial(attend_kernel, heads),
        out_shape=(
            struct(n, heads * HD),
            struct(n, HD),
            struct(n, HD),
            struct(n, heads * HD),
            struct(8, n, dtype=f32),
        ),
        cost_estimate=pl.CostEstimate(
            flops=heads * n * n * HD * 3, bytes_accessed=n * HD * 60, transcendentals=heads * n * n
        ),
    )(qkv, bias, cosine, sine)


def attend_back(heads, q, k, v, lse, do, cosine, sine):
    n = SEQ_LEN
    return pl.pallas_call(
        functools.partial(attend_back_kernel, heads),
        out_shape=(struct(n, (heads + 2) * HD), struct(1, (heads + 2) * HD, dtype=f32)),
        scratch_shapes=[pltpu.VMEM((n, HD), f32), pltpu.VMEM((n, HD), f32)],
        cost_estimate=pl.CostEstimate(
            flops=heads * n * n * HD * 7, bytes_accessed=n * HD * 60, transcendentals=heads * n * n
        ),
    )(q, k, v, lse, do, cosine, sine)


def gather_sequence(rows, rank):
    y = swap(rows, "tensor", 1)
    c = swap(rows, "tensor", 0)
    cy = swap(y, "tensor", 0)
    full = place([(0, rows), (2, y), (1, c), (3, cy)], 4, rank)
    return full.reshape(4 * rows.shape[0], rows.shape[1])


def scatter_sequence(left, right, rank):
    core, y = rank % 2, rank // 2
    blocks = left.reshape(2, 2, left.shape[0] // 4, left.shape[1])
    rows = blocks.shape[2]
    away = pick(blocks, 1 - core, 1).reshape(2 * rows, -1)
    here = pick(blocks, core, 1)
    came = swap(mm_nt(away, right).astype(bf16), "tensor", 0).reshape(2, rows, -1)
    across = mm_nt(pick(here, 1 - y, 0), right) + pick(came, 1 - y, 0).astype(f32)
    came_y = swap(across.astype(bf16), "tensor", 1)
    own = mm_nt(pick(here, y, 0), right) + pick(came, y, 0).astype(f32)
    return own + came_y.astype(f32)


def gather_group(rows):
    half = rows.shape[0] // 2
    y = swap(rows, "tensor", 1)
    z = swap(rows, "dp", LOW)
    yz = jnp.concatenate([swap(y[:half], "dp", LOW), swap(z[half:], "tensor", 1)], 0)
    mine = [rows, y, z, yz]
    return jnp.concatenate(mine + [swap(a, "tensor", 0) for a in mine], 0)


def scatter_group(product, rows):
    half = rows // 2
    came = swap(product(4 * rows, 4 * rows).astype(bf16), "tensor", 0)
    kept = product(0, 4 * rows) + came.astype(f32)
    own, y, z, yz = (kept[i * rows : (i + 1) * rows] for i in range(4))
    yz_top = swap(yz[:half].astype(bf16), "dp", LOW).astype(f32)
    yz_low = swap(yz[half:].astype(bf16), "tensor", 1).astype(f32)
    z_top = swap(z[:half].astype(bf16), "dp", LOW).astype(f32)
    y_low = swap(y[half:].astype(bf16), "tensor", 1).astype(f32)
    y_top = swap((y[:half] + yz_top).astype(bf16), "tensor", 1).astype(f32)
    z_low = swap((z[half:] + yz_low).astype(bf16), "dp", LOW).astype(f32)
    return own + jnp.concatenate([y_top + z_top, y_low + z_low], 0)


def shards(
    tokens,
    cotangent,
    norm1_gain,
    query_weight,
    query_bias,
    key_weight,
    key_bias,
    value_weight,
    value_bias,
    out_weight,
    norm2_gain,
    gate_weight,
    up_weight,
    down_weight,
):
    count = lax.axis_size("dp")
    levels = count.bit_length() - 1
    rank, part = lax.axis_index("tensor"), lax.axis_index("dp")
    core, y = rank % 2, rank // 2
    low = (part >> LOW) & 1
    high_bits = list(range(2, levels))
    heads = H // 4
    width = heads * HD
    head_kv = rank * heads // (H // KV)
    model = tokens.shape[1]
    rows = tokens.shape[0]
    block = query_weight.shape[0]
    slim = key_weight.shape[0]
    slim_kv = key_bias.shape[0]

    vector = jnp.concatenate([query_bias, key_bias, value_bias, norm1_gain, norm2_gain])
    pad_rows = -slim % 16 + 16
    small = jnp.concatenate(
        [
            jnp.concatenate([key_weight, value_weight], 1),
            jnp.pad(vector[None], ((0, pad_rows - 1), (0, 2 * KV * HD - vector.shape[0]))),
        ],
        0,
    )
    small_y = swap(small, "tensor", 1)
    small_c = swap(small, "tensor", 0)
    small_cy = swap(small_y, "tensor", 0)
    small = place([(0, small), (2, small_y), (1, small_c), (3, small_cy)], 4, rank)
    pair = small[:, :slim].reshape(block, 2 * KV * HD)
    vectors = small[:, slim]
    cut = [0, slim, slim + slim_kv, slim + 2 * slim_kv, 2 * slim + 2 * slim_kv, 3 * slim + 2 * slim_kv]
    qbias, kbias, vbias, gain1, gain2 = (
        vectors[:, cut[i] : cut[i + 1]].reshape(-1) for i in range(5)
    )
    gain1 = gain1.astype(f32)[:, None]
    gain2 = gain2.astype(f32)[:, None]
    raw_qkv = jnp.concatenate(
        [
            query_weight,
            lax.dynamic_slice_in_dim(pair, head_kv * HD, HD, 1),
            lax.dynamic_slice_in_dim(pair, (KV + head_kv) * HD, HD, 1),
        ],
        1,
    )
    bias_row = jnp.concatenate([qbias, kbias, vbias])
    span = width + 2 * HD
    qkv_block = jnp.concatenate(
        [
            (raw_qkv.astype(f32) * gain1).astype(bf16),
            jnp.pad(bias_row[None], ((0, 15), (0, span - bias_row.shape[0]))),
        ],
        0,
    )
    attention_bits = high_bits + [1, 0]
    qkv_blocks = place(spread(qkv_block, "dp", attention_bits), count, part)
    out_blocks = place(spread(out_weight.T, "dp", attention_bits), count, part)
    qkv_full = qkv_blocks[:, :block].reshape(model, span)
    out_full = out_blocks.reshape(model, width)
    bias_all = qkv_blocks[:, block].astype(f32)
    quarter = 4 * slim_kv
    qbias_all = bias_all[:, :block].reshape(-1)
    kbias_all = bias_all[:, block : block + quarter].reshape(-1)
    vbias_all = bias_all[:, block + quarter : block + 2 * quarter].reshape(-1)
    bias = jnp.concatenate(
        [
            lax.dynamic_slice_in_dim(qbias_all, rank * width, width, 0),
            lax.dynamic_slice_in_dim(kbias_all, head_kv * HD, HD, 0),
            lax.dynamic_slice_in_dim(vbias_all, head_kv * HD, HD, 0),
        ]
    )[None]

    x = tokens.astype(f32)
    r1 = lax.rsqrt(jnp.mean(x * x, axis=-1, keepdims=True) + epsilon)
    n1_all = gather_sequence((x * r1).astype(bf16), rank)
    cosine, sine = rope_tables()
    q, k, v, mixed, lse = attend(heads, mm(n1_all, qkv_full), bias, cosine, sine)
    h1 = x + scatter_sequence(mixed, out_full, rank)
    r2 = lax.rsqrt(jnp.mean(h1 * h1, axis=-1, keepdims=True) + epsilon)

    units = gate_weight.shape[1]
    half_units = (units + 255) // 256 * 128
    fringe = 2 * half_units - units

    def fetch(shard):
        halves = jnp.pad(shard, ((0, 0), (0, fringe)))
        keep = lax.dynamic_slice_in_dim(halves, low * half_units, half_units, 1)
        give = lax.dynamic_slice_in_dim(halves, (1 - low) * half_units, half_units, 1)
        blocks = [(0, keep), (1 << LOW, swap(give, "dp", LOW))]
        for bit in high_bits + [0]:
            blocks = blocks + [(o ^ (1 << bit), swap(b, "dp", bit)) for o, b in blocks]
        return place(blocks, count, part).reshape(model, half_units)

    gate_full = fetch((gate_weight.astype(f32) * gain2).astype(bf16))
    up_full = fetch((up_weight.astype(f32) * gain2).astype(bf16))
    down_full = fetch(down_weight.T)

    grad_all = gather_group(cotangent)
    n2_all = gather_group((h1 * r2).astype(bf16))
    gate_vals = mm(n2_all, gate_full)
    up_vals = mm(n2_all, up_full)
    sig = jax.nn.sigmoid(gate_vals)
    swish = gate_vals * sig
    activated = (swish * up_vals).astype(bf16)
    act_grad = mm(grad_all, down_full)
    gate_grad = (act_grad * up_vals * (sig * (1.0 + gate_vals * (1.0 - sig)))).astype(bf16)
    up_grad = (act_grad * swish).astype(bf16)

    def e2_rows(first, size):
        return mm_nt(gate_grad[first : first + size], gate_full) + mm_nt(
            up_grad[first : first + size], up_full
        )

    e2 = scatter_group(e2_rows, rows)

    def reduce_weight(grad):
        value = grad.astype(bf16).reshape((2,) * levels + (block, half_units))
        names = list(range(levels - 1, -1, -1))
        for bit in [0] + high_bits[::-1]:
            mine = (part >> bit) & 1
            axis = names.index(bit)
            came = swap(pick(value, 1 - mine, axis).astype(bf16), "dp", bit)
            value = pick(value, mine, axis).astype(f32) + came.astype(f32)
            names.remove(bit)
        came = swap(pick(value, 1 - low, 0).astype(bf16), "dp", LOW).astype(f32)
        own = pick(value, low, 0)
        full = jnp.concatenate(
            [jnp.where(low == 0, own, came), jnp.where(low == 0, came, own)], 1
        )
        return full[:, :units]

    gate_raw = reduce_weight(mm_tn(n2_all, gate_grad))
    up_raw = reduce_weight(mm_tn(n2_all, up_grad))
    down_raw = reduce_weight(mm_tn(grad_all, activated))
    output = h1 + scatter_group(
        lambda first, size: mm_nt(activated[first : first + size], down_full), rows
    )

    upstream = cotangent.astype(f32)
    dh1 = upstream + r2 * e2 - h1 * (r2**3 * jnp.mean(e2 * h1, axis=-1, keepdims=True))
    dh_all = gather_sequence(dh1.astype(bf16), rank)
    mixed_grad = mm(dh_all, out_full).astype(bf16)
    dqkv, bias_grad = attend_back(heads, q, k, v, lse, mixed_grad, cosine, sine)
    e1 = scatter_sequence(dqkv, qkv_full, rank)
    tokens_grad = dh1 + r1 * e1 - x * (r1**3 * jnp.mean(e1 * x, axis=-1, keepdims=True))

    qb_full = lax.dynamic_update_slice_in_dim(
        jnp.zeros((H * HD,), f32), bias_grad[0, :width], rank * width, 0
    )
    kb_full = lax.dynamic_update_slice_in_dim(
        jnp.zeros((KV * HD,), f32), bias_grad[0, width : width + HD], head_kv * HD, 0
    )
    vb_full = lax.dynamic_update_slice_in_dim(
        jnp.zeros((KV * HD,), f32), bias_grad[0, width + HD :], head_kv * HD, 0
    )
    bias_rows = jnp.concatenate(
        [v_.reshape(count, -1) for v_ in (qb_full, kb_full, vb_full)], 1
    ).astype(bf16)
    bias_rows = jnp.pad(bias_rows[:, None], ((0, 0), (0, 15), (0, span - bias_rows.shape[1])))
    qkv_grad = jnp.concatenate(
        [mm_tn(n1_all, dqkv).astype(bf16).reshape(count, block, span), bias_rows], 1
    )
    out_grad = mm_tn(dh_all, mixed).astype(bf16).reshape(count, block, width)

    def reduce_blocks(value):
        value = value.reshape((2,) * levels + value.shape[1:])
        names = list(range(levels - 1, -1, -1))
        for bit in attention_bits[::-1]:
            mine = (part >> bit) & 1
            axis = names.index(bit)
            came = swap(pick(value, 1 - mine, axis).astype(bf16), "dp", bit)
            value = pick(value, mine, axis).astype(f32) + came.astype(f32)
            names.remove(bit)
        return value

    out_shard = reduce_blocks(out_grad).T
    qkv_raw = reduce_blocks(qkv_grad)
    bias_sum = qkv_raw[block]
    qkv_raw = qkv_raw[:block]
    gain1_part = jnp.sum(qkv_raw * raw_qkv.astype(f32), axis=1)
    gain2_part = jnp.sum(gate_raw * gate_weight.astype(f32), axis=1) + jnp.sum(
        up_raw * up_weight.astype(f32), axis=1
    )

    vectors = jnp.concatenate(
        [
            bias_sum[:block].reshape(4, slim),
            bias_sum[block : block + quarter].reshape(4, slim_kv),
            bias_sum[block + quarter : block + 2 * quarter].reshape(4, slim_kv),
            gain1_part.reshape(4, slim),
            gain2_part.reshape(4, slim),
        ],
        1,
    )
    pair = jnp.zeros((block, 2 * KV * HD), f32)
    pair = lax.dynamic_update_slice_in_dim(pair, qkv_raw[:, width : width + HD], head_kv * HD, 1)
    pair = lax.dynamic_update_slice_in_dim(
        pair, qkv_raw[:, width + HD :], (KV + head_kv) * HD, 1
    )
    last = jnp.concatenate(
        [
            pair.reshape(4, slim, 2 * KV * HD),
            jnp.pad(
                vectors[:, None], ((0, 0), (0, 7), (0, 2 * KV * HD - vectors.shape[1]))
            ),
        ],
        1,
    ).reshape((2, 2, slim + 8, 2 * KV * HD))
    came = swap(pick(last, 1 - core, 1), "tensor", 0)
    last = pick(last, core, 1) + came
    came = swap(pick(last, 1 - y, 0), "tensor", 1)
    last = pick(last, y, 0) + came
    own_gain = norm1_gain.astype(f32)[:, None]
    tail = last[slim]
    return (
        output,
        tokens_grad,
        tail[cut[3] : cut[4]],
        qkv_raw[:, :width] * gain1,
        tail[cut[0] : cut[1]],
        last[:slim, : KV * HD] * own_gain,
        tail[cut[1] : cut[2]],
        last[:slim, KV * HD :] * own_gain,
        tail[cut[2] : cut[3]],
        out_shard,
        tail[cut[4] : cut[5]],
        gate_raw * gain2,
        up_raw * gain2,
        down_raw.T,
    )


def solution(mesh):
    both = ("dp", "tensor")
    rows, vector = P(both, None), P(both)
    return jax.shard_map(
        shards,
        mesh=mesh,
        in_specs=(
            rows,
            rows,
            vector,
            P("dp", "tensor"),
            vector,
            rows,
            vector,
            rows,
            vector,
            P("tensor", "dp"),
            vector,
            P("dp", "tensor"),
            P("dp", "tensor"),
            P("tensor", "dp"),
        ),
        out_specs=(
            rows,
            rows,
            vector,
            P("dp", "tensor"),
            vector,
            rows,
            vector,
            rows,
            vector,
            P("tensor", "dp"),
            vector,
            P("dp", "tensor"),
            P("dp", "tensor"),
            P("tensor", "dp"),
        ),
        check_vma=False,
    )
```

```python
import functools

import jax
import jax.numpy as jnp
from jax import lax
from jax.experimental import pallas as pl
from jax.experimental.pallas import tpu as pltpu
from jax.sharding import PartitionSpec as P

H = 12
KV = 2
HD = 128
SEQ_LEN = 1024
BLOCK = 256

epsilon = 1e-06
rope_base = 1000000.0
bf16 = jnp.bfloat16
f32 = jnp.float32
MESH = pl.DeviceIdType.MESH


LOW = 1


def swap(value, axis, bit):
    size = lax.axis_size(axis)
    return lax.ppermute(value, axis, [(i, i ^ (1 << bit)) for i in range(size)])


def mm(a, b):
    return jnp.dot(a, b, preferred_element_type=f32)


def mm_tn(a, b):
    return lax.dot_general(a, b, (((0,), (0,)), ((), ())), preferred_element_type=f32)


def mm_nt(a, b):
    return lax.dot_general(a, b, (((1,), (1,)), ((), ())), preferred_element_type=f32)


def pick(value, index, axis):
    return lax.dynamic_index_in_dim(value, index, axis, keepdims=False)


def after(value, *needed):
    return lax.optimization_barrier((value,) + needed)[0]


def join(own, came, bit, axis):
    low = jnp.where(bit == 0, own, came)
    high = jnp.where(bit == 0, came, own)
    return jnp.stack([low, high], axis)


def bit_of(index, bit):
    return (index >> bit) & 1


def rope_tables():
    positions = lax.iota(f32, SEQ_LEN)
    frequency = rope_base ** (-(lax.iota(f32, HD // 2) * 2.0) / HD)
    angles = positions[:, None] * frequency[None, :]
    cosine, sine = jnp.cos(angles), jnp.sin(angles)
    return jnp.concatenate([cosine, cosine], -1), jnp.concatenate([-sine, sine], -1)


def attend_back_kernel(
    heads, q_ref, k_ref, v_ref, lse_ref, do_ref, cos_ref, sin_ref, d_ref, bias_ref, dk, dv
):
    factor = HD**-0.5
    cosine, sine = cos_ref[...], sin_ref[...]
    k_turned = k_ref[...].T
    dk[...] = jnp.zeros_like(dk)
    dv[...] = jnp.zeros_like(dv)
    qsum = [jnp.zeros((1, HD), f32) for _ in range(heads)]
    for i in range(SEQ_LEN // BLOCK):
        rows = slice(i * BLOCK, (i + 1) * BLOCK)
        keys = (i + 1) * BLOCK
        for h in range(heads):
            cols = slice(h * HD, (h + 1) * HD)
            q, do = q_ref[rows, cols], do_ref[rows, cols]
            scores = mm_nt(k_ref[:keys, :], q) * factor
            probs = jnp.exp(scores - lse_ref[h : h + 1, rows])
            dv[:keys, :] += mm(probs.astype(bf16), do)
            dp = mm_nt(v_ref[:keys, :], do)
            delta = jnp.sum(probs * dp, axis=0, keepdims=True)
            ds = (probs * (dp - delta)).astype(bf16)
            dk[:keys, :] += mm(ds, q)
            w = mm(k_turned[:, :keys], ds).T * factor
            w = w * cosine[rows, :] - pltpu.roll(w, HD // 2, 1) * sine[rows, :]
            qsum[h] = qsum[h] + jnp.sum(w, axis=0, keepdims=True)
            d_ref[rows, cols] = w.astype(bf16)
    for h in range(heads):
        bias_ref[:, h * HD : (h + 1) * HD] = qsum[h]
    w = dk[...] * factor
    w = w * cosine - pltpu.roll(w, HD // 2, 1) * sine
    last = heads * HD
    d_ref[:, last : last + HD] = w.astype(bf16)
    bias_ref[:, last : last + HD] = jnp.sum(w, axis=0, keepdims=True)
    d_ref[:, last + HD : last + 2 * HD] = dv[...].astype(bf16)
    bias_ref[:, last + HD : last + 2 * HD] = jnp.sum(dv[...], axis=0, keepdims=True)


def struct(*shape, dtype=bf16):
    return jax.ShapeDtypeStruct(shape, dtype)


def attend_back(heads, q, k, v, lse, do, cosine, sine):
    n = SEQ_LEN
    return pl.pallas_call(
        functools.partial(attend_back_kernel, heads),
        out_shape=(struct(n, (heads + 2) * HD), struct(1, (heads + 2) * HD, dtype=f32)),
        scratch_shapes=[pltpu.VMEM((n, HD), f32), pltpu.VMEM((n, HD), f32)],
        cost_estimate=pl.CostEstimate(
            flops=heads * n * n * HD * 7, bytes_accessed=n * HD * 60, transcendentals=heads * n * n
        ),
    )(q, k, v, lse, do, cosine, sine)


def gather_tensor(own, rank):
    y = swap(own, "tensor", 1)
    c = swap(own, "tensor", 0)
    cy = swap(y, "tensor", 0)
    core, across = bit_of(rank, 0), bit_of(rank, 1)
    return join(join(own, c, core, 0), join(y, cy, core, 0), across, 0).reshape((4,) + own.shape)


def gather_sequence(rows, rank):
    return gather_tensor(rows, rank).reshape(4 * rows.shape[0], rows.shape[1])


class Link:
    def __init__(self, part, rank, sent, got):
        self.part, self.rank, self.sent, self.got, self.copies = part, rank, sent, got, []

    def device(self, where):
        kind, bit = where
        if kind == "dp":
            return {"dp": self.part ^ bit, "tensor": self.rank}
        return {"dp": self.part, "tensor": self.rank ^ bit}

    def meet(self, wheres):
        barrier = pltpu.get_barrier_semaphore()
        for where in wheres:
            pl.semaphore_signal(barrier, 1, device_id=self.device(where), device_id_type=MESH)
        pl.semaphore_wait(barrier, len(wheres))

    def send(self, src, dst, where):
        k = len(self.copies)
        copy = pltpu.make_async_remote_copy(
            src_ref=src,
            dst_ref=dst,
            send_sem=self.sent.at[k],
            recv_sem=self.got.at[k],
            device_id=self.device(where),
            device_id_type=MESH,
        )
        copy.start()
        self.copies.append(copy)
        return copy

    def sent_out(self, copy):
        copy.wait_send()
        self.copies = [other if other is not copy else None for other in self.copies]

    def finish(self):
        for copy in self.copies:
            if copy is not None:
                copy.wait_send()


class Local:
    def __init__(self, sems):
        self.sems, self.k = sems, 0

    def start(self, src, dst):
        copy = pltpu.make_async_copy(src, dst, self.sems.at[self.k])
        copy.start()
        self.k += 1
        return copy


Y, CORE = ("tensor", 2), ("tensor", 1)
X, ZLO = ("dp", 1), ("dp", 2)


def flat_row(values, width):
    n = values.shape[0]
    total = n * width
    lane = lax.broadcasted_iota(jnp.int32, (width, total), 1)
    spread = jnp.where(lane % width == lax.broadcasted_iota(jnp.int32, (width, total), 0), 1.0, 0.0)
    wide = mm(values.astype(bf16), spread.astype(bf16))
    mask = lax.broadcasted_iota(jnp.int32, (n, total), 1) // width == lax.broadcasted_iota(
        jnp.int32, (n, total), 0
    )
    return jnp.sum(jnp.where(mask, wide, 0.0), axis=0, keepdims=True)


def forward_kernel(count, heads, slim, slim_kv, *refs):
    (
        x_ref, n1_ref, small_ref, query_ref, out_ref, gate_ref, up_ref, down_ref, grad_ref, cos_ref, sin_ref,
        n1_out, small_out, wq_out, wkv_out, wo_out, gate_full, up_full, down_full, grad_all, n2_all,
        q_ref, k_ref, v_ref, o_ref, lse_ref, h1_ref, gains_ref,
        n1_all, small_all, wq, wkv, wo, own, pieces, qkv, away, came, across, came_y, n2, grad_own, vectors,
        local_sems, sent, got,
    ) = refs
    rank, part = lax.axis_index("tensor"), lax.axis_index("dp")
    core, y, low = rank % 2, rank // 2, (part // 2) % 2
    levels = count.bit_length() - 1
    high = [1 << bit for bit in range(2, levels)]
    rows = n1_ref.shape[0]
    block = query_ref.shape[0]
    half = gate_full.shape[1]
    link, local = Link(part, rank, sent, got), Local(local_sems)
    head_kv = rank * heads // (H // KV)
    link.meet([("dp", o) for o in range(1, count)] + [Y, CORE])

    def at(ref, dp):
        return ref.at[pl.ds(pl.multiple_of(dp * block, 16), block), :]

    def rows_of(ref, tensor):
        return ref.at[pl.ds(pl.multiple_of(tensor * rows, 16), rows), :]

    class Spread:
        def __init__(self, source, full):
            self.source, self.full, self.moves, self.first = source, full, {}, {}

        def block(self, offset):
            return self.source if offset == 0 else at(self.full, part ^ offset)

        def send(self, offset, where):
            self.moves[(offset, where)] = link.send(
                self.block(offset), at(self.full, part ^ offset), where
            )

        def wait(self, offset, where):
            self.moves[(offset, where)].wait_recv()

        def hop(self, offsets, where):
            for o in offsets:
                self.send(o, where)

        def arrive(self, offsets, where):
            for o in offsets:
                self.wait(o, where)

    def subsets(bits):
        out = [0]
        for bit in bits:
            out = out + [o ^ bit for o in out]
        return out

    query, out = Spread(query_ref, wq), Spread(out_ref, wo)

    class Feed(Spread):
        def __init__(self, source, full):
            super().__init__(source.at[:, pl.ds(pl.multiple_of(low * half, 128), half)], full)
            self.padded = source

        def give(self):
            self.moves[(0, ZLO)] = link.send(
                self.padded.at[:, pl.ds(pl.multiple_of((1 - low) * half, 128), half)],
                at(self.full, part),
                ZLO,
            )

    gate, up, down = Feed(gate_ref, gate_full), Feed(up_ref, up_full), Feed(down_ref, down_full)

    n1_y = link.send(n1_ref, rows_of(n1_all, rank), Y)
    n1_c = link.send(n1_ref, rows_of(n1_all, rank), CORE)
    smalls = [link.send(small_ref, small_all.at[rank, part], ("dp", o)) for o in range(count - 1, 0, -1)]
    if high:
        query.hop([0], ("dp", high[0]))
    gate.give()
    gate.send(0, X)
    own_n1 = local.start(n1_ref, rows_of(n1_all, rank))
    own_small = local.start(small_ref, small_all.at[rank, part])
    own_q = local.start(query_ref, at(wq, part))
    own_o = local.start(out_ref, at(wo, part))
    own_feed = [
        local.start(f.source, own.at[i]) for i, f in enumerate((gate, up, down))
    ]
    own_grad = local.start(grad_ref, grad_own)
    for i, bit in enumerate(high):
        query.arrive(subsets(high[:i]), ("dp", bit))
        if i + 1 < len(high):
            query.hop(subsets(high[: i + 1]), ("dp", high[i + 1]))
    query.hop(subsets(high), ZLO)
    if high:
        out.hop([0], ("dp", high[0]))
        gate.send(0, ("dp", high[0]))
    own_small.wait()
    for copy in smalls:
        copy.wait_recv()
    small_y = link.send(small_all.at[rank], small_all.at[rank], Y)
    small_c = link.send(small_all.at[rank], small_all.at[rank], CORE)
    query.arrive(subsets(high), ZLO)
    query.hop(subsets(high + [2]), X)
    for i, bit in enumerate(high):
        out.arrive(subsets(high[:i]), ("dp", bit))
        if i + 1 < len(high):
            out.hop(subsets(high[: i + 1]), ("dp", high[i + 1]))
    out.hop(subsets(high), ZLO)
    up.give()
    gate.wait(0, ZLO)
    gate.send(2, X)
    if high:
        gate.send(2, ("dp", high[0]))
        up.send(0, ("dp", high[0]))
    small_y.wait_recv()
    small_cy = link.send(small_all.at[rank ^ 2], small_all.at[rank ^ 2], CORE)
    n1_y.wait_recv()
    n1_cy = link.send(rows_of(n1_all, rank ^ 2), rows_of(n1_all, rank ^ 2), CORE)
    grad_y = link.send(grad_ref, grad_all.at[1], Y)
    out.arrive(subsets(high), ZLO)
    out.hop(subsets(high + [2]), X)
    down.give()
    for copy in own_feed:
        copy.wait()
    own_feed = [local.start(own.at[i], at(f.full, part)) for i, f in enumerate((gate, up, down))]
    own_grad.wait()
    own_grad = local.start(grad_own, grad_all.at[0])
    up.send(0, X)
    small_c.wait_recv()
    small_cy.wait_recv()

    outs = [local.start(small_all, small_out)]
    cut = [0, slim, slim + slim_kv, slim + 2 * slim_kv, 2 * slim + 2 * slim_kv, 3 * slim + 2 * slim_kv]
    for j in range(count):
        for t in range(4):
            vectors[4 * j + t : 4 * j + t + 1, :] = small_all[t, j, slim : slim + 1, : 2 * HD].astype(f32)
            for kind in range(2):
                first = pl.multiple_of((KV * kind + head_kv) * HD, 128)
                pieces[j * block + t * slim : j * block + (t + 1) * slim, kind * HD : (kind + 1) * HD] = (
                    small_all[t, j, :slim, pl.ds(first, HD)]
                )
    gain1 = flat_row(vectors[:, cut[3] : cut[4]], slim)
    gains_ref[0:1, :] = gain1
    gains_ref[1:2, :] = flat_row(vectors[:, cut[4] : cut[5]], slim)
    gains_ref[2:3, :] = flat_row(vectors[:, cut[0] : cut[1]], slim)
    gains_ref[3:4, : KV * HD] = flat_row(vectors[:, cut[1] : cut[2]], slim_kv)
    gains_ref[4:5, : KV * HD] = flat_row(vectors[:, cut[2] : cut[3]], slim_kv)
    width = heads * HD
    bias_q = gains_ref[2:3, pl.ds(pl.multiple_of(rank * width, 128), width)]
    bias_k = gains_ref[3:4, pl.ds(pl.multiple_of(head_kv * HD, 128), HD)]
    bias_v = gains_ref[4:5, pl.ds(pl.multiple_of(head_kv * HD, 128), HD)]
    outs.append(local.start(pieces, wkv_out))
    own_n1.wait()
    n1_c.wait_recv()
    n1_cy.wait_recv()
    link.sent_out(n1_cy)
    own_q.wait()
    query.arrive(subsets(high + [2]), X)
    outs.append(local.start(wq, wq_out))

    cosine_ref, sine_ref = cos_ref, sin_ref
    for i in range(SEQ_LEN // BLOCK):
        r = slice(i * BLOCK, (i + 1) * BLOCK)
        n = (n1_all[r, :].astype(f32) * gain1).astype(bf16)
        n1_all[r, :] = n
        cosine, sine = cosine_ref[r, :], sine_ref[r, :]
        zq = mm(n, wq[...]) + bias_q
        zk = mm(n, pieces[...])
        for h in range(heads + 1):
            z = zq[:, h * HD : (h + 1) * HD] if h < heads else zk[:, :HD] + bias_k
            z = (z * cosine + pltpu.roll(z, HD // 2, 1) * sine).astype(bf16)
            if h < heads:
                q_ref[r, h * HD : (h + 1) * HD] = z
            else:
                k_ref[r, :] = z
        v_ref[r, :] = (zk[:, HD:] + bias_v).astype(bf16)
    outs.append(local.start(n1_all, n1_out))
    grad_z = link.send(grad_ref, grad_all.at[2], ZLO)
    up.wait(0, ZLO)
    if high:
        gate.wait(0, ("dp", high[0]))
        gate.send(high[0], X)
        up.send(2, ("dp", high[0]))
    up.send(2, X)

    factor = HD**-0.5
    v_turned = v_ref[...].T
    for i in range(SEQ_LEN // BLOCK):
        r = slice(i * BLOCK, (i + 1) * BLOCK)
        keys = (i + 1) * BLOCK
        for h in range(heads):
            cols = slice(h * HD, (h + 1) * HD)
            scores = mm_nt(k_ref[:keys, :], q_ref[r, cols]) * factor
            top = jnp.max(scores, axis=0, keepdims=True)
            grown = jnp.exp(scores - top)
            total = jnp.sum(grown, axis=0, keepdims=True)
            probs = (grown * (1.0 / total)).astype(bf16)
            o_ref[r, cols] = mm(v_turned[:, :keys], probs).T.astype(bf16)
            lse_ref[h : h + 1, r] = top + jnp.log(total)

    own_o.wait()
    out.arrive(subsets(high + [2]), X)
    outs.append(local.start(wo, wo_out))

    def project(block_index):
        return mm_nt(o_ref[pl.ds(pl.multiple_of(block_index * rows, 16), rows), :], wo[...])

    for j in range(2):
        away[j] = project(2 * j + 1 - core).astype(bf16)
    to_core = link.send(away, came, CORE)
    if high:
        gate.wait(2, ("dp", high[0]))
        gate.send(high[0] ^ 2, X)
        down.send(0, ("dp", high[0]))
    down.wait(0, ZLO)
    down.send(0, X)
    to_core.wait_recv()
    across[...] = (project(2 * (1 - y) + core) + came[1 - y].astype(f32)).astype(bf16)
    to_y = link.send(across, came_y, Y)
    h1 = project(2 * y + core) + came[y].astype(f32) + x_ref[...].astype(f32)
    if high:
        up.wait(0, ("dp", high[0]))
        up.send(high[0], X)
        down.send(2, ("dp", high[0]))
    down.send(2, X)
    to_y.wait_recv()
    h1 = h1 + came_y[...].astype(f32)
    h1_ref[...] = h1
    r2 = lax.rsqrt(jnp.mean(h1 * h1, axis=-1, keepdims=True) + epsilon)
    n2[...] = (h1 * r2 * gains_ref[1:2, :]).astype(bf16)

    top, bottom = pl.ds(0, rows // 2), pl.ds(rows // 2, rows // 2)
    outs.append(local.start(n2, n2_all.at[0]))
    n2_y = link.send(n2, n2_all.at[1], Y)
    n2_z = link.send(n2, n2_all.at[2], ZLO)
    n2_c = link.send(n2, n2_all.at[4], CORE)
    grad_c = link.send(grad_ref, grad_all.at[4], CORE)
    if high:
        up.wait(2, ("dp", high[0]))
        up.send(high[0] ^ 2, X)
    grad_y.wait_recv()
    grad_yz = link.send(grad_all.at[1, top], grad_all.at[3, top], ZLO)
    grad_yc = link.send(grad_all.at[1], grad_all.at[5], CORE)
    n2_y.wait_recv()
    n2_yz = link.send(n2_all.at[1, top], n2_all.at[3, top], ZLO)
    n2_yc = link.send(n2_all.at[1], n2_all.at[5], CORE)
    n2_z.wait_recv()
    n2_zy = link.send(n2_all.at[2, bottom], n2_all.at[3, bottom], Y)
    n2_zc = link.send(n2_all.at[2], n2_all.at[6], CORE)
    grad_z.wait_recv()
    grad_zy = link.send(grad_all.at[2, bottom], grad_all.at[3, bottom], Y)
    grad_zc = link.send(grad_all.at[2], grad_all.at[6], CORE)
    if high:
        down.wait(0, ("dp", high[0]))
        down.send(high[0], X)
    n2_yz.wait_recv()
    n2_zy.wait_recv()
    n2_yzc = link.send(n2_all.at[3], n2_all.at[7], CORE)
    grad_yz.wait_recv()
    grad_zy.wait_recv()
    grad_yzc = link.send(grad_all.at[3], grad_all.at[7], CORE)
    if high:
        down.wait(2, ("dp", high[0]))
        down.send(high[0] ^ 2, X)
    for bit, before in zip(high[1:], range(1, len(high))):
        for feed in (gate, up, down):
            held = subsets([2] + high[:before])
            feed.hop(held, ("dp", bit))
            feed.arrive(held, ("dp", bit))
            feed.hop([o ^ bit for o in held], X)
    for feed in (gate, up, down):
        for offset, where in feed.moves:
            if where == X:
                feed.wait(offset, where)
    for copy in (n2_c, n2_yc, n2_zc, n2_yzc, grad_c, grad_yc, grad_zc, grad_yzc):
        copy.wait_recv()
    for copy in own_feed + [own_grad] + outs:
        copy.wait()
    link.finish()


def forward(count, heads, slim, slim_kv, half_units, x, n1, small, query, out, gate, up, down, grad, cosine, sine):
    rows, model = n1.shape
    block = query.shape[0]
    width = heads * HD
    anywhere, vmem = pl.BlockSpec(memory_space=pl.ANY), pl.BlockSpec(memory_space=pltpu.VMEM)
    n = SEQ_LEN
    full = struct(model, half_units)
    group = struct(8, rows, model)
    copies = 3 + (count - 1) + 3 + 2 * (count - 1) + 3 * count + 2 + 18
    return pl.pallas_call(
        functools.partial(forward_kernel, count, heads, slim, slim_kv),
        name="forward",
        out_shape=(
            struct(n, model),
            struct(4, count, *small.shape),
            struct(model, width),
            struct(model, 2 * HD),
            struct(model, width),
            full,
            full,
            full,
            group,
            group,
            struct(n, width),
            struct(n, HD),
            struct(n, HD),
            struct(n, width),
            struct(8, n, dtype=f32),
            struct(rows, model, dtype=f32),
            struct(8, model, dtype=f32),
        ),
        in_specs=[vmem] + [anywhere] * 8 + [vmem] * 2,
        out_specs=(anywhere,) * 10 + (vmem,) * 7,
        scratch_shapes=[
            pltpu.VMEM((n, model), bf16),
            pltpu.VMEM((4, count) + small.shape, bf16),
            pltpu.VMEM((model, width), bf16),
            pltpu.VMEM((8, 128), bf16),
            pltpu.VMEM((model, width), bf16),
            pltpu.VMEM((3, block, half_units), bf16),
            pltpu.VMEM((model, 2 * HD), bf16),
            pltpu.VMEM((8, 128), f32),
            pltpu.VMEM((2, rows, model), bf16),
            pltpu.VMEM((2, rows, model), bf16),
            pltpu.VMEM((rows, model), bf16),
            pltpu.VMEM((rows, model), bf16),
            pltpu.VMEM((rows, model), bf16),
            pltpu.VMEM((rows, model), bf16),
            pltpu.VMEM((4 * count, 2 * HD), f32),
            pltpu.SemaphoreType.DMA((24,)),
            pltpu.SemaphoreType.DMA((copies,)),
            pltpu.SemaphoreType.DMA((copies,)),
        ],
        compiler_params=pltpu.CompilerParams(collective_id=0, has_side_effects=True),
    )(x, n1, small, query, out, gate, up, down, grad, cosine, sine)


def scatter_sequence(left, right, rank):
    core, y = rank % 2, rank // 2
    blocks = left.reshape(2, 2, left.shape[0] // 4, left.shape[1])
    rows = blocks.shape[2]
    away = pick(blocks, 1 - core, 1).reshape(2 * rows, -1)
    here = pick(blocks, core, 1)
    came = swap(mm_nt(away, right).astype(bf16), "tensor", 0).reshape(2, rows, -1)
    across = mm_nt(pick(here, 1 - y, 0), right) + pick(came, 1 - y, 0).astype(f32)
    came_y = swap(across.astype(bf16), "tensor", 1)
    own = mm_nt(pick(here, y, 0), right) + pick(came, y, 0).astype(f32)
    return own + came_y.astype(f32)


def gather_group(rows):
    half = rows.shape[0] // 2
    y = swap(rows, "tensor", 1)
    z = swap(rows, "dp", LOW)
    yz = jnp.concatenate([swap(y[:half], "dp", LOW), swap(z[half:], "tensor", 1)], 0)
    mine = [rows, y, z, yz]
    return jnp.concatenate(mine + [swap(a, "tensor", 0) for a in mine], 0)


def scatter_group(product, rows):
    half = rows // 2
    came = swap(product(4 * rows, 4 * rows).astype(bf16), "tensor", 0)
    kept = product(0, 4 * rows) + came.astype(f32)
    own, y, z, yz = (kept[i * rows : (i + 1) * rows] for i in range(4))
    yz_top = swap(yz[:half].astype(bf16), "dp", LOW).astype(f32)
    yz_low = swap(yz[half:].astype(bf16), "tensor", 1).astype(f32)
    z_top = swap(z[:half].astype(bf16), "dp", LOW).astype(f32)
    y_low = swap(y[half:].astype(bf16), "tensor", 1).astype(f32)
    y_top = swap((y[:half] + yz_top).astype(bf16), "tensor", 1).astype(f32)
    z_low = swap((z[half:] + yz_low).astype(bf16), "dp", LOW).astype(f32)
    return own + jnp.concatenate([y_top + z_top, y_low + z_low], 0), kept


def shards(
    tokens,
    cotangent,
    norm1_gain,
    query_weight,
    query_bias,
    key_weight,
    key_bias,
    value_weight,
    value_bias,
    out_weight,
    norm2_gain,
    gate_weight,
    up_weight,
    down_weight,
):
    count = lax.axis_size("dp")
    levels = count.bit_length() - 1
    rank, part = lax.axis_index("tensor"), lax.axis_index("dp")
    core, y = bit_of(rank, 0), bit_of(rank, 1)
    low = bit_of(part, LOW)
    high_bits = list(range(2, levels))
    heads = H // 4
    width = heads * HD
    head_kv = rank * heads // (H // KV)
    model = tokens.shape[1]
    rows = tokens.shape[0]
    block = query_weight.shape[0]
    slim = key_weight.shape[0]
    slim_kv = key_bias.shape[0]

    attention_bits = high_bits + [1, 0]

    units = gate_weight.shape[1]
    half_units = (units + 255) // 256 * 128

    def padded(shard):
        return jnp.pad(shard, ((0, 0), (0, 2 * half_units - units)))

    vector = jnp.concatenate([query_bias, key_bias, value_bias, norm1_gain, norm2_gain])
    pad_rows = -slim % 16 + 16
    small = jnp.concatenate(
        [
            jnp.concatenate([key_weight, value_weight], 1),
            jnp.pad(vector[None], ((0, pad_rows - 1), (0, 2 * KV * HD - vector.shape[0]))),
        ],
        0,
    )
    x = tokens.astype(f32)
    r1 = lax.rsqrt(jnp.mean(x * x, axis=-1, keepdims=True) + epsilon)
    cosine, sine = rope_tables()
    (
        n1_all, small_all, wq, wkv, out_full, gate_full, up_full, down_full, grad_all, n2_all,
        q, k, v, mixed, lse, h1, gains,
    ) = forward(
        count, heads, slim, slim_kv, half_units, tokens, (x * r1).astype(bf16), small, query_weight,
        out_weight.T, padded(gate_weight), padded(up_weight), padded(down_weight.T), cotangent, cosine, sine,
    )
    grad_all = grad_all.reshape(8 * rows, model)
    n2_all = n2_all.reshape(8 * rows, model)
    gain1_all, gain2_all = gains[0], gains[1]
    gain1 = lax.dynamic_slice_in_dim(gain1_all, part * block, block, 0)
    gain2 = lax.dynamic_slice_in_dim(gain2_all, part * block, block, 0)
    raw_kv = lax.dynamic_slice_in_dim(wkv, part * block, block, 0)
    qkv_full = jnp.concatenate([wq, wkv], 1)
    span = width + 2 * HD
    quarter = 4 * slim_kv
    cut = [0, slim, slim + slim_kv, slim + 2 * slim_kv, 2 * slim + 2 * slim_kv, 3 * slim + 2 * slim_kv]
    r2 = lax.rsqrt(jnp.mean(h1 * h1, axis=-1, keepdims=True) + epsilon)

    gate_vals = mm(n2_all, gate_full)
    up_vals = mm(n2_all, up_full)
    sig = jax.nn.sigmoid(gate_vals)
    swish = gate_vals * sig
    activated = (swish * up_vals).astype(bf16)
    down_product = mm_tn(grad_all, activated).astype(bf16)
    act_grad = mm(after(grad_all, down_product), down_full)
    gate_grad = (act_grad * up_vals * (sig * (1.0 + gate_vals * (1.0 - sig)))).astype(bf16)
    up_grad = (act_grad * swish).astype(bf16)

    class Reduce:
        def __init__(self, grad, bits):
            self.value = grad.reshape((2,) * levels + grad.shape[1:])
            self.names = list(range(levels - 1, -1, -1))
            self.bits = list(bits)
            self.split = bits[-1] == LOW
            self.send()

        def send(self):
            bit = self.bits[0]
            away = pick(self.value, 1 - bit_of(part, bit), self.names.index(bit))
            self.came = swap(away.astype(bf16), "dp", bit)

        def step(self, *needed):
            bit = self.bits.pop(0)
            came = after(self.came, *needed) if needed else self.came
            came = came.astype(f32)
            own = pick(self.value, bit_of(part, bit), self.names.index(bit)).astype(f32)
            if self.split and bit == LOW:
                both = jnp.where(low == 0, own, came), jnp.where(low == 0, came, own)
                self.value = jnp.concatenate(both, 1)[:, :units]
                return self.value
            self.value = own + came
            self.names.remove(bit)
            if self.bits:
                self.send()
            if len(self.bits) > 2:
                return self.step()
            return self.value

    feed_bits = [0] + high_bits[::-1] + [LOW]

    def feed_reduce(product):
        return Reduce(product.reshape(count, block, half_units), feed_bits)

    down_sum = feed_reduce(down_product)
    e2_sum, e2_kept = scatter_group(
        lambda first, size: mm_nt(gate_grad[first : first + size], gate_full)
        + mm_nt(up_grad[first : first + size], up_full),
        rows,
    )
    gate_sum = feed_reduce(mm_tn(n2_all, after(gate_grad, e2_kept)).astype(bf16))
    down_sum.step(e2_kept)
    up_sum = feed_reduce(mm_tn(n2_all, after(up_grad, gate_sum.value)).astype(bf16))
    e2 = e2_sum * gain2_all

    upstream = cotangent.astype(f32)
    dh1 = upstream + r2 * e2 - h1 * (r2**3 * jnp.mean(e2 * h1, axis=-1, keepdims=True))
    dh_low = dh1.astype(bf16)
    dh_all = gather_sequence(dh_low, rank)
    gate_sum.step(dh_low)
    out_sum, _ = scatter_group(
        lambda first, size: mm_nt(after(activated, dh_low)[first : first + size], down_full), rows
    )
    output = h1 + out_sum
    out_grad = mm_tn(dh_all, mixed).astype(bf16)
    mixed_grad = mm(after(dh_all, out_grad), out_full).astype(bf16)
    out_grads = Reduce(out_grad.reshape(count, block, width), attention_bits[::-1])
    down_sum.step(mixed_grad)
    dqkv, bias_grad = attend_back(heads, q, k, v, lse, mixed_grad, cosine, sine)

    qb_full = lax.dynamic_update_slice_in_dim(
        jnp.zeros((H * HD,), f32), bias_grad[0, :width], rank * width, 0
    )
    kb_full = lax.dynamic_update_slice_in_dim(
        jnp.zeros((KV * HD,), f32), bias_grad[0, width : width + HD], head_kv * HD, 0
    )
    vb_full = lax.dynamic_update_slice_in_dim(
        jnp.zeros((KV * HD,), f32), bias_grad[0, width + HD :], head_kv * HD, 0
    )
    bias_rows = jnp.concatenate(
        [v_.reshape(count, -1) for v_ in (qb_full, kb_full, vb_full)], 1
    ).astype(bf16)
    bias_rows = jnp.pad(bias_rows[:, None], ((0, 0), (0, 15), (0, span - bias_rows.shape[1])))
    qkv_grads = Reduce(
        jnp.concatenate(
            [mm_tn(n1_all, dqkv).astype(bf16).reshape(count, block, span), bias_rows], 1
        ),
        attention_bits[::-1],
    )
    e1 = scatter_sequence(after(dqkv, qkv_grads.value), qkv_full, rank) * gain1_all
    tokens_grad = dh1 + r1 * e1 - x * (r1**3 * jnp.mean(e1 * x, axis=-1, keepdims=True))
    up_sum.step(qkv_grads.value)
    out_grads.step(qkv_grads.value)
    stage = qkv_grads.step()
    gate_sum.step(stage)
    down_out = down_sum.step(stage)
    out_grads.step(stage)
    stage = qkv_grads.step(tokens_grad)
    out_shard = out_grads.step(stage).T
    up_sum.step(stage)
    gate_out = gate_sum.step(stage)
    qkv_raw = qkv_grads.step()
    up_out = up_sum.step(qkv_raw)

    bias_sum = qkv_raw[block]
    qkv_raw = qkv_raw[:block]
    gain1_part = jnp.sum(qkv_raw[:, :width] * query_weight.astype(f32), axis=1) + jnp.sum(
        qkv_raw[:, width:] * raw_kv.astype(f32), axis=1
    )
    gain1_part = gain1_part / gain1
    gain2_part = (
        jnp.sum(gate_out * gate_weight.astype(f32), axis=1)
        + jnp.sum(up_out * up_weight.astype(f32), axis=1)
    ) / gain2

    vectors = jnp.concatenate(
        [
            bias_sum[:block].reshape(4, slim),
            bias_sum[block : block + quarter].reshape(4, slim_kv),
            bias_sum[block + quarter : block + 2 * quarter].reshape(4, slim_kv),
            gain1_part.reshape(4, slim),
            gain2_part.reshape(4, slim),
        ],
        1,
    )
    pair = jnp.zeros((block, 2 * KV * HD), f32)
    pair = lax.dynamic_update_slice_in_dim(pair, qkv_raw[:, width : width + HD], head_kv * HD, 1)
    pair = lax.dynamic_update_slice_in_dim(
        pair, qkv_raw[:, width + HD :], (KV + head_kv) * HD, 1
    )
    last = jnp.concatenate(
        [
            pair.reshape(4, slim, 2 * KV * HD),
            jnp.pad(vectors[:, None], ((0, 0), (0, 7), (0, 2 * KV * HD - vectors.shape[1]))),
        ],
        1,
    ).reshape((2, 2, slim + 8, 2 * KV * HD))
    came = swap(pick(last, 1 - core, 1), "tensor", 0)
    last = pick(last, core, 1) + came
    came = swap(pick(last, 1 - y, 0), "tensor", 1)
    last = pick(last, y, 0) + came
    tail = last[slim]
    return (
        output,
        tokens_grad,
        tail[cut[3] : cut[4]],
        qkv_raw[:, :width],
        tail[cut[0] : cut[1]],
        last[:slim, : KV * HD],
        tail[cut[1] : cut[2]],
        last[:slim, KV * HD :],
        tail[cut[2] : cut[3]],
        out_shard,
        tail[cut[4] : cut[5]],
        gate_out,
        up_out,
        down_out.T,
    )


def solution(mesh):
    both = ("dp", "tensor")
    rows, vector = P(both, None), P(both)
    return jax.shard_map(
        shards,
        mesh=mesh,
        in_specs=(
            rows,
            rows,
            vector,
            P("dp", "tensor"),
            vector,
            rows,
            vector,
            rows,
            vector,
            P("tensor", "dp"),
            vector,
            P("dp", "tensor"),
            P("dp", "tensor"),
            P("tensor", "dp"),
        ),
        out_specs=(
            rows,
            rows,
            vector,
            P("dp", "tensor"),
            vector,
            rows,
            vector,
            rows,
            vector,
            P("tensor", "dp"),
            vector,
            P("dp", "tensor"),
            P("dp", "tensor"),
            P("tensor", "dp"),
        ),
        check_vma=False,
    )
```
